32 devices in a mesh: groups: 2 (over y), tensor: 16 (over z, x, core).
Axes of the slice: x: 2, y: 2, z: 4, core: 2. Of those that a mesh axis runs over, the one named last changes fastest.
Arguments:
- inputs: bfloat16 [256, 8192], P('groups', 'tensor'), parts along dimension 0, may hold values from -6 to 6
- gate_weight: bfloat16 [8192, 28672], P(None, 'tensor'), may hold values from -0.09375 to 0.09375
- up_weight: bfloat16 [8192, 28672], P(None, 'tensor'), may hold values from -0.09375 to 0.09375
- down_weight: bfloat16 [28672, 8192], P('tensor'), may hold values from -0.03125 to 0.03125
- cotangent: bfloat16 [4, 256, 8192], P(None, 'groups', 'tensor'), parts along dimension 1, may hold values from -6 to 6
- threshold_levels: int32 [28672], P('tensor'), may hold values from 4 to 16
- membrane_offsets: int32 [256, 28672], P('groups', 'tensor'), parts along dimension 0, may hold values from 0 to 255
Outputs:
- grad_input: float32 [256, 8192], P('groups', 'tensor'), parts along dimension 0
- grad_threshold: float32 [57344], P(('groups', 'tensor')), parts along dimension 0
The draws below stay inside these ranges and needn't reach their ends.
There are 2 independent parts, one for each index of `groups`. The reference program is written for one: setup_inputs(seed, part) draws one part's arguments, and reference() takes and returns one part's arrays. A program takes and returns all parts, laid end to end along the dimension named above; an argument that names none is the same for every part. Nothing has to cross between parts.
All inputs are finite; a program needn't handle non-finite values.
Results may differ from the reference program's by a relative error of at most 0.0031.
Values may be sent and summed in bfloat16 or wider, within the bound.
No kernel may reach another device: no remote copies, remote signals or barrier semaphores. Data moves between devices by JAX's collectives and lax.ppermute only.
A program may use at most 256 MiB of HBM per device.

```python
import jax
import jax.numpy as jnp
from jax import lax

D = 8192
FF = 28672
TOK = 128
STEPS = 4


def with_ends(result, own_key, smallest, largest):
    index_at = [jax.random.randint(jax.random.fold_in(own_key, axis), (), 0, length) for axis, length in enumerate(result.shape)]
    longest = result.shape.index(max(result.shape))
    neighbour = index_at[:longest] + [(index_at[longest] + 1) % result.shape[longest]] + index_at[longest + 1:]
    return result.at[tuple(index_at)].set(smallest).at[tuple(neighbour)].set(largest)


def with_spikes(array, stream_key, source, target, shards_of, factor):
    owner, partner = [(jnp.arange(array.shape[dim]) // (array.shape[dim] // shards_of)).reshape([-1 if axis == dim else 1 for axis in range(array.ndim)]) for dim in (source, target)]
    chosen = jax.random.permutation(stream_key, shards_of)[partner]
    strong = (owner == chosen) | (owner == (partner + shards_of // 2) % shards_of)
    return jnp.where(strong, factor * array, array)


def levels(stream_key, dims, pieces, smallest, top_value):
    level, own = 1.0, jax.random.fold_in(stream_key, 6)
    for axis_at, blocks in pieces:
        heights = jnp.exp(jax.random.uniform(jax.random.fold_in(own, axis_at), (blocks,), jnp.float32, smallest / len(pieces), top_value / len(pieces)))
        level = level * jnp.repeat(heights, dims[axis_at] // blocks).reshape([-1 if axis == axis_at else 1 for axis in range(len(dims))])
    return level


def bell_draw(stream_key, shape, scale, bound, cuts=(), dtype=jnp.bfloat16):
    values = scale * jax.random.normal(stream_key, shape, jnp.float32)
    if cuts:
        values = values * levels(stream_key, shape, cuts, -0.22, 0.18)
    return jnp.clip(values, -bound, bound).astype(dtype)


def heavy_noise(stream_key, extent, width, limit, shards, heavy, kind=jnp.bfloat16):
    array = width * jax.random.normal(stream_key, extent, jnp.float32)
    if shards:
        array = array * levels(stream_key, extent, shards, -0.22, 0.18)
    return jnp.clip(with_spikes(array, jax.random.fold_in(stream_key, 3), *heavy), -limit, limit).astype(kind)


def setup_inputs(seed: int = 0, part: int = 0) -> dict:
    arg_keys = jax.random.split(jax.random.key(seed), 8)
    part_splits = jax.random.split(jax.random.fold_in(arg_keys[7], part), 8)
    inputs = bell_draw(part_splits[0], (TOK, D), 1.0, 6.0, ((1, 16),))
    gate_weight = heavy_noise(arg_keys[1], (D, FF), D ** -0.5, 0.09375, ((1, 16),), (1, 0, 16, 2.0))
    up_weight = heavy_noise(arg_keys[2], (D, FF), D ** -0.5, 0.09375, ((1, 16),), (1, 0, 16, 2.0))
    down_weight = bell_draw(arg_keys[3], (FF, D), FF ** -0.5, 0.03125, ((0, 16),))
    cotangent = bell_draw(part_splits[4], (STEPS, TOK, D), 1.0, 6.0, ((2, 16),))
    threshold_levels = with_ends(jax.random.randint(arg_keys[5], (FF,), 4, 17), jax.random.fold_in(arg_keys[5], 1), 4, 16).astype(jnp.int32)
    membrane_offsets = with_ends(jax.random.randint(part_splits[6], (TOK, FF), 0, 256), jax.random.fold_in(part_splits[6], 1), 0, 255).astype(jnp.int32)
    return dict(inputs=inputs, gate_weight=gate_weight, up_weight=up_weight, down_weight=down_weight, cotangent=cotangent, threshold_levels=threshold_levels, membrane_offsets=membrane_offsets)


slope_gain = 4.0


def transposed_product(left, weight):
    return lax.dot_general(left, weight, (((1,), (1,)), ((), ())), preferred_element_type=jnp.float32)


def reference(inputs, gate_weight, up_weight, down_weight, cotangent, threshold_levels, membrane_offsets):
    gate = jnp.dot(inputs, gate_weight, preferred_element_type=jnp.float32)
    up = jnp.dot(inputs, up_weight, preferred_element_type=jnp.float32)
    theta = threshold_levels.astype(jnp.float32) / 8.0
    sig = jax.nn.sigmoid(gate)
    current = gate * sig * up
    dsilu = sig * (1.0 + gate * (1.0 - sig))
    offset_share = membrane_offsets.astype(jnp.float32) / 256.0
    membrane = theta * offset_share
    spikes = []
    for step in range(STEPS):
        pre = membrane + current
        spike = jax.nn.sigmoid(slope_gain * (pre - theta))
        spikes.append(spike)
        membrane = pre - theta * spike
    later = jnp.zeros_like(current)
    grad_threshold = jnp.zeros(theta.shape, jnp.float32)
    grad_input = jnp.zeros((inputs.shape[0], inputs.shape[1]), jnp.float32)
    for step in range(STEPS - 1, -1, -1):
        feedback = transposed_product(cotangent[step], down_weight)
        spike = spikes[step]
        dspike = theta * (feedback - later)
        slope = slope_gain * spike * (1.0 - spike)
        dpre = dspike * slope + later
        grad_threshold = grad_threshold + jnp.sum(feedback * spike - later * spike - dspike * slope, axis=0)
        dgate = (dpre * up * dsilu).astype(jnp.bfloat16)
        dup = (dpre * gate * sig).astype(jnp.bfloat16)
        grad_input = grad_input + transposed_product(dgate, gate_weight) + transposed_product(dup, up_weight)
        later = dpre
    grad_threshold = grad_threshold + jnp.sum(later * offset_share, axis=0)
    return grad_input, grad_threshold
```

```python
import jax
import jax.numpy as jnp
from jax import lax
from jax.experimental import pallas as pl
from jax.experimental.pallas import tpu as pltpu
from jax.sharding import PartitionSpec as P

slope_gain = 4.0
AXIS = "tensor"
NT = (((1,), (1,)), ((), ()))
F32 = jnp.float32
BF16 = jnp.bfloat16
VMEM_LIMIT = 48 << 20


def nt_dot(left, weight):
    return lax.dot_general(left, weight, NT, preferred_element_type=F32)


def dot(left, right):
    return jnp.dot(left, right, preferred_element_type=F32)


def forward_call(tok, pairs, blocks, gate_w, up_w, down_w, sums):
    count = len(pairs)
    rows, width = pairs[0][0].shape
    hidden = gate_w.shape[1]
    first = sums is None
    pieces = [piece for pair in pairs for piece in pair]

    def kernel(blk, *refs):
        data = refs[: 2 * count]
        ga, gb, ua, ub, da, db = refs[2 * count : 2 * count + 6]
        rest = refs[2 * count + 6 :]
        gate, up, feed = rest[-3:]
        at = pl.program_id(0)
        for j in range(count):

            @pl.when(at == j)
            def _(j=j):
                own, other = data[2 * j], data[2 * j + 1]
                fresh = first and j == 0
                xo = own[rows - tok :, :]
                xp = other[rows - tok :, :]
                g = dot(xo, ga[...]) + dot(xp, gb[...])
                u = dot(xo, ua[...]) + dot(xp, ub[...])
                if fresh:
                    gate[...] = g
                    up[...] = u
                elif j == 0:
                    gate[...] = rest[0][...] + g
                    up[...] = rest[1][...] + u
                else:
                    gate[...] += g
                    up[...] += u
                f = nt_dot(own[: rows - tok, :], da[...]) + nt_dot(other[: rows - tok, :], db[...])
                if fresh:
                    feed[...] = f
                elif j == 0:
                    feed[...] = rest[2][...] + f
                else:
                    feed[...] += f

    whole = lambda shape: pl.BlockSpec(shape, lambda j, b: (0, 0))
    spec = lambda k: pl.BlockSpec((width, hidden), lambda j, b: (b[k, j], 0))
    dspec = lambda k: pl.BlockSpec((hidden, width), lambda j, b: (0, b[k, j]))
    sum_shapes = [(tok, hidden), (tok, hidden), (rows - tok, hidden)]
    in_specs = [whole((rows, width)) for _ in pieces]
    in_specs += [spec(0), spec(1), spec(0), spec(1), dspec(0), dspec(1)]
    args = pieces + [gate_w, gate_w, up_w, up_w, down_w, down_w]
    aliases = {}
    if not first:
        aliases = {1 + len(args) + k: k for k in range(3)}
        in_specs += [whole(s) for s in sum_shapes]
        args += list(sums)
    return pl.pallas_call(
        kernel,
        grid_spec=pltpu.PrefetchScalarGridSpec(
            num_scalar_prefetch=1,
            grid=(count,),
            in_specs=in_specs,
            out_specs=[whole(s) for s in sum_shapes],
        ),
        out_shape=[jax.ShapeDtypeStruct(s, F32) for s in sum_shapes],
        input_output_aliases=aliases,
        compiler_params=pltpu.CompilerParams(vmem_limit_bytes=VMEM_LIMIT),
        cost_estimate=pl.CostEstimate(
            flops=2 * count * 2 * width * hidden * (rows + tok),
            transcendentals=0,
            bytes_accessed=2 * count * width * (6 * hidden + 2 * rows),
        ),
        name="forward",
    )(blocks, *args)


def neuron_call(gate, up, feed, levels, offsets):
    tok, hidden = gate.shape
    steps = feed.shape[0] // tok
    part = 256 if hidden % 256 == 0 else hidden
    tile = 16

    def kernel(gate_ref, up_ref, feed_ref, lev_ref, off_ref, dg_ref, du_ref, gt_ref):
        theta = jnp.broadcast_to(lev_ref[...].astype(F32) / 8.0, (tile, part))

        def step_rows(r, acc):
            at = pl.ds(pl.multiple_of(r * tile, tile), tile)
            g = gate_ref[at, :]
            u = up_ref[at, :]
            sig = jax.nn.sigmoid(g)
            gs = g * sig
            current = gs * u
            dsilu = sig * (1.0 + g * (1.0 - sig))
            share = off_ref[at, :].astype(F32) / 256.0
            membrane = theta * share
            spikes = []
            for _ in range(steps):
                pre = membrane + current
                spike = jax.nn.sigmoid(slope_gain * (pre - theta))
                spikes.append(spike)
                membrane = pre - theta * spike
            later = jnp.zeros_like(current)
            usl = u * dsilu
            dgate = jnp.zeros_like(current)
            dup = jnp.zeros_like(current)
            for t in range(steps - 1, -1, -1):
                fb = feed_ref[pl.ds(pl.multiple_of(t * tok + r * tile, tile), tile), :]
                spike = spikes[t]
                diff = fb - later
                slope = slope_gain * spike * (1.0 - spike)
                both = theta * diff * slope
                dpre = both + later
                acc = acc + (diff * spike - both)
                dgate = dgate + (dpre * usl).astype(BF16).astype(F32)
                dup = dup + (dpre * gs).astype(BF16).astype(F32)
                later = dpre
            dg_ref[at, :] = dgate.astype(BF16)
            du_ref[at, :] = dup.astype(BF16)
            return acc + later * share

        acc = lax.fori_loop(0, tok // tile, step_rows, jnp.zeros((tile, part), F32))
        gt_ref[...] = jnp.sum(acc, axis=0, keepdims=True)

    col = lambda rows: pl.BlockSpec((rows, part), lambda s: (0, s))
    return pl.pallas_call(
        kernel,
        grid=(hidden // part,),
        in_specs=[col(tok), col(tok), col(steps * tok), col(1), col(tok)],
        out_specs=[col(tok), col(tok), col(1)],
        out_shape=[
            jax.ShapeDtypeStruct((tok, hidden), BF16),
            jax.ShapeDtypeStruct((tok, hidden), BF16),
            jax.ShapeDtypeStruct((1, hidden), F32),
        ],
        cost_estimate=pl.CostEstimate(
            flops=120 * tok * hidden, transcendentals=10 * tok * hidden, bytes_accessed=32 * tok * hidden
        ),
        name="neuron",
    )(gate, up, feed, levels.reshape(1, hidden), offsets)


def backward_call(dgate, dup, blocks, count, gate_w, up_w, width):
    tok, hidden = dgate.shape

    def kernel(blk, dg, du, ga, gb, ua, ub, own, other):
        own[0] = nt_dot(dg[...], ga[...]) + nt_dot(du[...], ua[...])
        other[0] = nt_dot(dg[...], gb[...]) + nt_dot(du[...], ub[...])

    whole = pl.BlockSpec((tok, hidden), lambda j, b: (0, 0))
    spec = lambda k: pl.BlockSpec((width, hidden), lambda j, b: (b[k, j], 0))
    out = pl.BlockSpec((1, tok, width), lambda j, b: (j, 0, 0))
    return pl.pallas_call(
        kernel,
        grid_spec=pltpu.PrefetchScalarGridSpec(
            num_scalar_prefetch=1,
            grid=(count,),
            in_specs=[whole, whole, spec(0), spec(1), spec(0), spec(1)],
            out_specs=[out, out],
        ),
        out_shape=[jax.ShapeDtypeStruct((count, tok, width), F32)] * 2,
        compiler_params=pltpu.CompilerParams(vmem_limit_bytes=VMEM_LIMIT),
        cost_estimate=pl.CostEstimate(
            flops=count * 8 * width * hidden * tok,
            transcendentals=0,
            bytes_accessed=count * width * (8 * hidden + 8 * tok),
        ),
        name="backward",
    )(blocks, dgate, dup, gate_w, gate_w, up_w, up_w)


def z_map(moves):
    return [(i, moves[i // 4] * 4 + i % 4) for i in range(16) if i // 4 in moves]


CORE = [(i, i ^ 1) for i in range(16)]
PAIR = z_map({0: 1, 1: 0, 2: 3, 3: 2})
MID = z_map({1: 2, 2: 1})
OUT = z_map({1: 0, 2: 3})
CROSS = [(i, i ^ 2) for i in range(16)]


def around(turn, flip):
    return [(i, ((i // 4 + turn) % 4 * 4 + i % 4) ^ (2 * flip)) for i in range(16)]


def send(piece, moves):
    return lax.ppermute(piece, AXIS, moves)


fence = lax.optimization_barrier


def body_line(inputs, gate_w, up_w, down_w, cotangent, levels, offsets):
    steps, tok, width = cotangent.shape
    me = lax.axis_index(AXIS)
    core = me % 2
    chip = me // 2
    z = me // 4
    middle = (z == 1) | (z == 2)

    def blocks_of(chips):
        chips = jnp.stack(chips).astype(jnp.int32)
        return jnp.stack([2 * chips + core, 2 * chips + 1 - core]).astype(jnp.int32)

    far_a = jnp.where(middle, 6, 4)
    far_b = jnp.where(middle, 4, 6)

    own = jnp.concatenate([cotangent.reshape(steps * tok, width), inputs], axis=0)
    x0 = send(own, CROSS)
    p1 = send(own, PAIR)
    p2a = send(own, MID)
    own_c = send(own, CORE)
    sums = forward_call(tok, [(own, own_c)], blocks_of([chip]), gate_w, up_w, down_w, None)
    x0, p1, p2a = fence((x0, p1, p2a))
    x1 = send(p1, CROSS)
    p2b = send(p1, MID)
    p3a = send(p2a, OUT)
    x0_c = send(x0, CORE)
    p1_c = send(p1, CORE)
    sums = forward_call(
        tok, [(x0, x0_c), (p1, p1_c)], blocks_of([chip ^ 1, chip ^ 2]), gate_w, up_w, down_w, sums
    )
    x1, p2b, p3a = fence((x1, p2b, p3a))
    a = jnp.where(middle, p2a, p3a)
    x2 = send(a, CROSS)
    p3b = send(p2b, OUT)
    x1_c = send(x1, CORE)
    a_c = send(a, CORE)
    sums = forward_call(
        tok, [(x1, x1_c), (a, a_c)], blocks_of([chip ^ 3, chip ^ far_a]), gate_w, up_w, down_w, sums
    )
    x2, p3b = fence((x2, p3b))
    b = jnp.where(middle, p2b, p3b)
    x3 = send(b, CROSS)
    x2_c = send(x2, CORE)
    b_c = send(b, CORE)
    sums = forward_call(
        tok, [(x2, x2_c), (b, b_c)], blocks_of([chip ^ 1 ^ far_a, chip ^ far_b]), gate_w, up_w, down_w, sums
    )
    x3_c = send(x3, CORE)
    sums = forward_call(tok, [(x3, x3_c)], blocks_of([chip ^ 1 ^ far_b]), gate_w, up_w, down_w, sums)

    dgate, dup, grad_threshold = neuron_call(*sums, levels, offsets)

    def dest(turn, flip):
        return ((z + turn) % 4 * 2 + chip % 2) ^ flip

    turns = [2, 1, 3]
    other_col = [dest(t, 1) for t in turns + [0]]
    mine1, theirs1 = backward_call(dgate, dup, blocks_of(other_col), 4, gate_w, up_w, width)
    got1 = send(theirs1, CORE)
    own_col = [dest(t, 0) for t in turns]
    mine2, theirs2 = backward_call(dgate, dup, blocks_of(own_col), 3, gate_w, up_w, width)
    got2 = send(theirs2, CORE)
    sum1 = (mine1 + got1).astype(BF16)
    parts = [send(sum1[k], around(t, 1)) for k, t in enumerate(turns + [0])]
    mine3, theirs3 = backward_call(dgate, dup, blocks_of([chip]), 1, gate_w, up_w, width)
    got3 = send(theirs3, CORE)
    sum2 = (mine2 + got2).astype(BF16)
    parts += [send(sum2[k], around(t, 0)) for k, t in enumerate(turns)]
    grad_input = mine3[0] + got3[0]
    for part in parts:
        grad_input = grad_input + part.astype(F32)
    return grad_input, grad_threshold.reshape(-1)


def body_plain(inputs, gate_w, up_w, down_w, cotangent, levels, offsets):
    steps, tok, width = cotangent.shape
    piece = lax.all_gather(inputs, AXIS, axis=1, tiled=True)
    gate = dot(piece, gate_w)
    up = dot(piece, up_w)
    cot = lax.all_gather(cotangent, AXIS, axis=2, tiled=True)
    feed = nt_dot(cot.reshape(steps * tok, -1), down_w)
    dgate, dup, grad_threshold = neuron_call(gate, up, feed, levels, offsets)
    term = nt_dot(dgate, gate_w) + nt_dot(dup, up_w)
    grad_input = lax.psum_scatter(term, AXIS, scatter_dimension=1, tiled=True)
    return grad_input, grad_threshold.reshape(-1)


def solution(mesh):
    placed = (
        P("groups", "tensor"),
        P(None, "tensor"),
        P(None, "tensor"),
        P("tensor", None),
        P(None, "groups", "tensor"),
        P("tensor"),
        P("groups", "tensor"),
    )
    body = body_line if mesh.shape[AXIS] == 16 else body_plain
    return jax.shard_map(
        body,
        mesh=mesh,
        in_specs=placed,
        out_specs=(P("groups", "tensor"), P(("groups", "tensor"))),
        check_vma=False,
    )
```

```python
import jax
import jax.numpy as jnp
from jax import lax
from jax.experimental import pallas as pl
from jax.experimental.pallas import tpu as pltpu
from jax.sharding import PartitionSpec as P

slope_gain = 4.0
AXIS = "tensor"
NT = (((1,), (1,)), ((), ()))
F32 = jnp.float32
BF16 = jnp.bfloat16
VMEM_LIMIT = 48 << 20


def nt_dot(left, weight):
    return lax.dot_general(left, weight, NT, preferred_element_type=F32)


def dot(left, right):
    return jnp.dot(left, right, preferred_element_type=F32)


def forward_call(tok, pairs, chips, core, gate_w, up_w, down_w, sums):
    count = len(pairs)
    rows, half = pairs[0][0].shape
    width = 2 * half
    hidden = gate_w.shape[1]
    slots = 2
    pieces = [piece for pair in pairs for piece in pair]
    sum_shapes = [(tok, hidden), (tok, hidden), (rows - tok, hidden)]
    carried = [] if sums is None else list(sums)
    where = jnp.stack([jnp.asarray(c, jnp.int32) for c in chips + [core]])

    def kernel(where_ref, *refs):
        data = refs[: 2 * count]
        weights = refs[2 * count : 2 * count + 3]
        old = refs[2 * count + 3 : 2 * count + 3 + len(carried)]
        new = refs[2 * count + 3 + len(carried) : 2 * count + 6 + len(carried)]
        feats, gbuf, ubuf, dbuf, gate, up, feed, dsem, wsem, ssem = refs[2 * count + 6 + len(carried) :]
        accs = (gate, up, feed)
        mine = pl.multiple_of(where_ref[count] * half, half)
        theirs = pl.multiple_of(half - where_ref[count] * half, half)

        def loads(i, slot):
            at = pl.multiple_of(where_ref[i] * width, width)
            return (
                pltpu.make_async_copy(weights[0].at[pl.ds(at, width), :], gbuf.at[slot], wsem.at[0, slot]),
                pltpu.make_async_copy(weights[1].at[pl.ds(at, width), :], ubuf.at[slot], wsem.at[1, slot]),
                pltpu.make_async_copy(weights[2].at[:, pl.ds(at, width)], dbuf.at[slot], wsem.at[2, slot]),
            )

        def data_loads(j, own, other):
            return (
                pltpu.make_async_copy(own, feats.at[j, :, pl.ds(mine, half)], dsem.at[0, j]),
                pltpu.make_async_copy(other, feats.at[j, :, pl.ds(theirs, half)], dsem.at[1, j]),
            )

        sums_in = [pltpu.make_async_copy(o, v, ssem.at[k]) for k, (o, v) in enumerate(zip(old, accs))]
        sums_out = [pltpu.make_async_copy(v, o, ssem.at[k]) for k, (v, o) in enumerate(zip(accs, new))]
        for copy in data_loads(0, data[0], data[1]):
            copy.start()
        for copy in loads(0, 0):
            copy.start()
        for copy in sums_in:
            copy.start()
        for j in range(1, count):
            for copy in data_loads(j, data[2 * j], data[2 * j + 1]):
                copy.start()
        if not carried:
            for acc in accs:
                acc[...] = jnp.zeros_like(acc)

        def step(i, _):
            slot = lax.rem(i, slots)

            @pl.when(i + 1 < count)
            def _():
                for copy in loads(i + 1, 1 - slot):
                    copy.start()

            for copy in data_loads(i, data[0], data[1]):
                copy.wait()
            arrived = loads(i, slot)
            for k, (acc, buf) in enumerate(zip(accs, (gbuf, ubuf, dbuf))):
                arrived[k].wait()
                if carried:

                    @pl.when(i == 0)
                    def _(k=k):
                        sums_in[k].wait()

                if k < 2:
                    acc[...] += dot(feats[i, rows - tok :, :], buf[slot])
                else:
                    acc[...] += nt_dot(feats[i, : rows - tok, :], buf[slot])

                @pl.when(i == count - 1)
                def _(k=k):
                    sums_out[k].start()

            return 0

        lax.fori_loop(0, count, step, 0)
        for copy in sums_out:
            copy.wait()

    any_spec = pl.BlockSpec(memory_space=pl.ANY)
    args = pieces + [gate_w, up_w, down_w] + carried
    return pl.pallas_call(
        kernel,
        in_specs=[pl.BlockSpec(memory_space=pltpu.SMEM)] + [any_spec] * len(args),
        out_specs=[any_spec] * 3,
        out_shape=[jax.ShapeDtypeStruct(s, F32) for s in sum_shapes],
        scratch_shapes=[
            pltpu.VMEM((count, rows, width), BF16),
            pltpu.VMEM((slots, width, hidden), BF16),
            pltpu.VMEM((slots, width, hidden), BF16),
            pltpu.VMEM((slots, hidden, width), BF16),
        ]
        + [pltpu.VMEM(s, F32) for s in sum_shapes]
        + [
            pltpu.SemaphoreType.DMA((2, count)),
            pltpu.SemaphoreType.DMA((3, slots)),
            pltpu.SemaphoreType.DMA((3,)),
        ],
        input_output_aliases={1 + 2 * count + 3 + k: k for k in range(3)} if carried else {},
        compiler_params=pltpu.CompilerParams(vmem_limit_bytes=VMEM_LIMIT),
        cost_estimate=pl.CostEstimate(
            flops=count * 2 * width * hidden * (rows + tok),
            transcendentals=0,
            bytes_accessed=count * width * (6 * hidden + 2 * rows),
        ),
        name="forward",
    )(where, *args)


def half_sigmoid(x):
    return 0.5 * jnp.tanh(x) + 0.5


def neuron_tile(theta, share, g, u, feeds):
    sig = half_sigmoid(0.5 * g)
    gs = g * sig
    current = gs * u
    usl = u * (sig * (1.0 + g * (1.0 - sig)))
    membrane = theta * share
    spikes = []
    for _ in feeds:
        pre = membrane + current
        spike = half_sigmoid((0.5 * slope_gain) * (pre - theta))
        spikes.append(spike)
        membrane = pre - theta * spike
    later = None
    for feed, spike in zip(feeds[::-1], spikes[::-1]):
        diff = feed if later is None else feed - later
        both = theta * diff * (slope_gain * spike * (1.0 - spike))
        dpre = both if later is None else both + later
        term = diff * spike - both
        dg = (dpre * usl).astype(BF16).astype(F32)
        du = (dpre * gs).astype(BF16).astype(F32)
        if later is None:
            grad, dgate, dup = term, dg, du
        else:
            grad, dgate, dup = grad + term, dgate + dg, dup + du
        later = dpre
    return dgate, dup, grad + later * share


def neuron_rows(gate, up, feed, lev_ref, off_ref, dg_ref, du_ref, gt_ref):
    tok, part = gate.shape
    steps = feed.shape[0] // tok
    tile = 16
    theta = jnp.broadcast_to(lev_ref[...].astype(F32) / 8.0, (tile, part))
    acc = jnp.zeros((tile, part), F32)
    for r in range(0, tok, tile):
        at = slice(r, r + tile)
        feeds = [feed[t * tok + r : t * tok + r + tile, :] for t in range(steps)]
        share = off_ref[at, :].astype(F32) / 256.0
        dgate, dup, grad = neuron_tile(theta, share, gate[at, :], up[at, :], feeds)
        dg_ref[at, :] = dgate.astype(BF16)
        du_ref[at, :] = dup.astype(BF16)
        acc = acc + grad
    gt_ref[...] = jnp.sum(acc, axis=0, keepdims=True)


def hidden_part(hidden):
    return 256 if hidden % 256 == 0 else hidden


def neuron_outs(tok, hidden):
    return [
        jax.ShapeDtypeStruct((tok, hidden), BF16),
        jax.ShapeDtypeStruct((tok, hidden), BF16),
        jax.ShapeDtypeStruct((1, hidden), F32),
    ]


def neuron_call(gate, up, feed, levels, offsets):
    tok, hidden = gate.shape
    part = hidden_part(hidden)
    col = lambda rows: pl.BlockSpec((rows, part), lambda s: (0, s))
    return pl.pallas_call(
        neuron_rows,
        grid=(hidden // part,),
        in_specs=[col(tok), col(tok), col(feed.shape[0]), col(1), col(tok)],
        out_specs=[col(tok), col(tok), col(1)],
        out_shape=neuron_outs(tok, hidden),
        name="neuron",
    )(gate, up, feed, levels.reshape(1, hidden), offsets)


def last_call(pair, blocks, gate_w, up_w, down_w, sums, levels, offsets):
    rows, width = pair[0].shape
    tok, hidden = sums[0].shape
    part = hidden_part(hidden)
    count = hidden // part

    def kernel(blk, own, other, ga, gb, ua, ub, da, db, gi, ui, fi, lev, off, dg, du, gt, gate, up, feed):
        now = lax.rem(pl.program_id(0), 2)
        neuron_rows(gate.at[1 - now], up.at[1 - now], feed.at[1 - now], lev, off, dg, du, gt)
        xo = own[rows - tok :, :]
        xp = other[rows - tok :, :]
        gate[now] = gi[...] + dot(xo, ga[...]) + dot(xp, gb[...])
        up[now] = ui[...] + dot(xo, ua[...]) + dot(xp, ub[...])
        feed[now] = fi[...] + nt_dot(own[: rows - tok, :], da[...]) + nt_dot(other[: rows - tok, :], db[...])

    ahead = lambda s: jnp.minimum(s, count - 1)
    behind = lambda s: jnp.maximum(s - 1, 0)
    whole = pl.BlockSpec((rows, width), lambda s, b: (0, 0))
    spec = lambda k: pl.BlockSpec((width, part), lambda s, b: (b[k, 0], ahead(s)))
    dspec = lambda k: pl.BlockSpec((part, width), lambda s, b: (ahead(s), b[k, 0]))
    col = lambda n: pl.BlockSpec((n, part), lambda s, b: (0, ahead(s)))
    late = lambda n: pl.BlockSpec((n, part), lambda s, b: (0, behind(s)))
    return pl.pallas_call(
        kernel,
        grid_spec=pltpu.PrefetchScalarGridSpec(
            num_scalar_prefetch=1,
            grid=(count + 1,),
            in_specs=[whole, whole, spec(0), spec(1), spec(0), spec(1), dspec(0), dspec(1)]
            + [col(tok), col(tok), col(rows - tok), late(1), late(tok)],
            out_specs=[late(tok), late(tok), late(1)],
            scratch_shapes=[
                pltpu.VMEM((2, tok, part), F32),
                pltpu.VMEM((2, tok, part), F32),
                pltpu.VMEM((2, rows - tok, part), F32),
            ],
        ),
        out_shape=neuron_outs(tok, hidden),
        compiler_params=pltpu.CompilerParams(vmem_limit_bytes=VMEM_LIMIT),
        name="last",
    )(blocks, *pair, gate_w, gate_w, up_w, up_w, down_w, down_w, *sums, levels.reshape(1, hidden), offsets)


def backward_call(dgate, dup, blocks, gate_w, up_w, width):
    tok, hidden = dgate.shape
    count = blocks.shape[0]
    slots = 3

    def kernel(blk, dg, du, gw, uw, out, gbuf, ubuf, sem):
        def loads(i, slot):
            at = pl.multiple_of(blk[i] * width, width)
            return (
                pltpu.make_async_copy(gw.at[pl.ds(at, width), :], gbuf.at[slot], sem.at[0, slot]),
                pltpu.make_async_copy(uw.at[pl.ds(at, width), :], ubuf.at[slot], sem.at[1, slot]),
            )

        for i in range(min(slots - 1, count)):
            for copy in loads(i, i):
                copy.start()

        def step(i, _):
            slot = lax.rem(i, slots)

            @pl.when(i + slots - 1 < count)
            def _():
                for copy in loads(i + slots - 1, lax.rem(i + slots - 1, slots)):
                    copy.start()

            for copy in loads(i, slot):
                copy.wait()
            out[i] = nt_dot(dg[...], gbuf[slot]) + nt_dot(du[...], ubuf[slot])
            return 0

        lax.fori_loop(0, count, step, 0)

    vmem = pl.BlockSpec(memory_space=pltpu.VMEM)
    any_spec = pl.BlockSpec(memory_space=pl.ANY)
    return pl.pallas_call(
        kernel,
        in_specs=[pl.BlockSpec(memory_space=pltpu.SMEM), vmem, vmem, any_spec, any_spec],
        out_specs=vmem,
        out_shape=jax.ShapeDtypeStruct((count, tok, width), F32),
        scratch_shapes=[
            pltpu.VMEM((slots, width, hidden), BF16),
            pltpu.VMEM((slots, width, hidden), BF16),
            pltpu.SemaphoreType.DMA((2, slots)),
        ],
        compiler_params=pltpu.CompilerParams(vmem_limit_bytes=VMEM_LIMIT),
        cost_estimate=pl.CostEstimate(
            flops=count * 4 * width * hidden * tok,
            transcendentals=0,
            bytes_accessed=count * width * (4 * hidden + 4 * tok),
        ),
        name="backward",
    )(blocks, dgate, dup, gate_w, up_w)


def z_map(moves):
    return [(i, moves[i // 4] * 4 + i % 4) for i in range(16) if i // 4 in moves]


CORE = [(i, i ^ 1) for i in range(16)]
PAIR = z_map({0: 1, 1: 0, 2: 3, 3: 2})
MID = z_map({1: 2, 2: 1})
OUT = z_map({1: 0, 2: 3})
CROSS = [(i, i ^ 2) for i in range(16)]


def around(turn, flip):
    return [(i, ((i // 4 + turn) % 4 * 4 + i % 4) ^ (2 * flip)) for i in range(16)]


def send(piece, moves):
    return lax.ppermute(piece, AXIS, moves)


fence = lax.optimization_barrier


def body_line(inputs, gate_w, up_w, down_w, cotangent, levels, offsets):
    steps, tok, width = cotangent.shape
    me = lax.axis_index(AXIS)
    core = me % 2
    chip = me // 2
    z = me // 4
    middle = (z == 1) | (z == 2)

    def blocks_of(chips):
        chips = jnp.stack(chips).astype(jnp.int32)
        return jnp.stack([2 * chips + core, 2 * chips + 1 - core]).astype(jnp.int32)

    far_a = jnp.where(middle, 6, 4)
    far_b = jnp.where(middle, 4, 6)

    own = jnp.concatenate([cotangent.reshape(steps * tok, width), inputs], axis=0)
    def more(pairs, chips, sums):
        return forward_call(tok, pairs, chips, core, gate_w, up_w, down_w, sums)

    p1 = send(own, PAIR)
    p2a = send(own, MID)
    x0 = send(own, CROSS)
    own_c = send(own, CORE)
    sums = more([(own, own_c)], [chip], None)
    x0, p1, p2a, sums = fence((x0, p1, p2a, sums))
    p2b = send(p1, MID)
    p3a = send(p2a, OUT)
    x1 = send(p1, CROSS)
    x0_c = send(x0, CORE)
    p1_c = send(p1, CORE)
    sums = more([(x0, x0_c), (p1, p1_c)], [chip ^ 1, chip ^ 2], sums)
    x1, p2a, p2b, p3a, sums = fence((x1, p2a, p2b, p3a, sums))
    a = jnp.where(middle, p2a, p3a)
    p3b = send(p2b, OUT)
    x2 = send(a, CROSS)
    x1_c = send(x1, CORE)
    a_c = send(a, CORE)
    sums = more([(x1, x1_c), (a, a_c)], [chip ^ 3, chip ^ far_a], sums)
    x2, p2b, p3b, sums = fence((x2, p2b, p3b, sums))
    b = jnp.where(middle, p2b, p3b)
    x3 = send(b, CROSS)
    x2_c = send(x2, CORE)
    b_c = send(b, CORE)
    sums = more([(x2, x2_c), (b, b_c)], [chip ^ 1 ^ far_a, chip ^ far_b], sums)
    x3, sums = fence((x3, sums))
    x3_c = send(x3, CORE)
    dgate, dup, grad_threshold = last_call(
        (x3, x3_c), blocks_of([chip ^ 1 ^ far_b]), gate_w, up_w, down_w, sums, levels, offsets
    )

    turns = [2, 1, 3, 0]

    def partial(dgate, dup, flip):
        chips = jnp.stack([((z + t) % 4 * 2 + chip % 2) ^ flip for t in turns]).astype(jnp.int32)
        out = backward_call(
            dgate, dup, jnp.concatenate([2 * chips + 1 - core, 2 * chips + core]), gate_w, up_w, width
        )
        return out[:4], out[4:]

    theirs, mine = partial(dgate, dup, 1)
    across = (mine + send(theirs, CORE)).astype(BF16)
    dgate, dup, across = fence((dgate, dup, across))
    across = send(across, CROSS)
    theirs, mine = partial(dgate, dup, 0)
    theirs, mine, across = fence((theirs, mine, across))
    column = mine + send(theirs, CORE) + across.astype(F32)
    grad_input = column[3]
    column = column.astype(BF16)
    for k in range(3):
        grad_input = grad_input + send(column[k], around(turns[k], 0)).astype(F32)
    return grad_input, grad_threshold.reshape(-1)


def body_plain(inputs, gate_w, up_w, down_w, cotangent, levels, offsets):
    steps, tok, width = cotangent.shape
    piece = lax.all_gather(inputs, AXIS, axis=1, tiled=True)
    gate = dot(piece, gate_w)
    up = dot(piece, up_w)
    cot = lax.all_gather(cotangent, AXIS, axis=2, tiled=True)
    feed = nt_dot(cot.reshape(steps * tok, -1), down_w)
    dgate, dup, grad_threshold = neuron_call(gate, up, feed, levels, offsets)
    term = nt_dot(dgate, gate_w) + nt_dot(dup, up_w)
    grad_input = lax.psum_scatter(term, AXIS, scatter_dimension=1, tiled=True)
    return grad_input, grad_threshold.reshape(-1)


def solution(mesh):
    placed = (
        P("groups", "tensor"),
        P(None, "tensor"),
        P(None, "tensor"),
        P("tensor", None),
        P(None, "groups", "tensor"),
        P("tensor"),
        P("groups", "tensor"),
    )
    body = body_line if mesh.shape[AXIS] == 16 else body_plain
    return jax.shard_map(
        body,
        mesh=mesh,
        in_specs=placed,
        out_specs=(P("groups", "tensor"), P(("groups", "tensor"))),
        check_vma=False,
    )
```

```python
import jax
import jax.numpy as jnp
from jax import lax
from jax.experimental import pallas as pl
from jax.experimental.pallas import tpu as pltpu
from jax.sharding import PartitionSpec as P

slope_gain = 4.0
AXIS = "tensor"
NT = (((1,), (1,)), ((), ()))
F32 = jnp.float32
BF16 = jnp.bfloat16


def nt_dot(left, weight):
    return lax.dot_general(left, weight, NT, preferred_element_type=F32)


def dot(left, right):
    return jnp.dot(left, right, preferred_element_type=F32)


def forward_call(tok, pairs, place, gate_w, up_w, down_w, sums):
    count = len(pairs)
    rows, half = pairs[0][0].shape
    width = 2 * half
    hidden = gate_w.shape[1]
    slots = 2
    pieces = [piece for pair in pairs for piece in pair]
    sum_shapes = [(tok, hidden), (tok, hidden), (rows - tok, hidden)]
    carried = [] if sums is None else list(sums)

    def kernel(*refs):
        me = lax.axis_index(AXIS)
        core = lax.rem(me, 2)
        chips = place(me)
        data = refs[: 2 * count]
        weights = refs[2 * count : 2 * count + 3]
        old = refs[2 * count + 3 : 2 * count + 3 + len(carried)]
        new = refs[2 * count + 3 + len(carried) : 2 * count + 6 + len(carried)]
        feats, gbuf, ubuf, dbuf, dsem, wsem = refs[2 * count + 6 + len(carried) :]
        gate, up, feed = new
        accs = (gate, feed, up)
        mine = pl.multiple_of(core * half, half)
        theirs = pl.multiple_of(half - core * half, half)

        def loads(i, slot):
            chip = chips[0]
            for j in range(1, count):
                chip = jnp.where(i == j, chips[j], chip)
            at = pl.multiple_of(chip * width, width)
            return (
                pltpu.make_async_copy(weights[0].at[pl.ds(at, width), :], gbuf.at[slot], wsem.at[0, slot]),
                pltpu.make_async_copy(weights[2].at[:, pl.ds(at, width)], dbuf.at[slot], wsem.at[2, slot]),
                pltpu.make_async_copy(weights[1].at[pl.ds(at, width), :], ubuf.at[slot], wsem.at[1, slot]),
            )

        def data_loads(j, own, other):
            return (
                pltpu.make_async_copy(own, feats.at[j, :, pl.ds(mine, half)], dsem.at[0, j]),
                pltpu.make_async_copy(other, feats.at[j, :, pl.ds(theirs, half)], dsem.at[1, j]),
            )

        for copy in data_loads(0, data[0], data[1]):
            copy.start()
        for copy in loads(0, 0):
            copy.start()
        for j in range(1, count):
            for copy in data_loads(j, data[2 * j], data[2 * j + 1]):
                copy.start()
        for k, acc in enumerate(new):
            acc[...] = old[k][...] if carried else jnp.zeros_like(acc)

        def step(i, _):
            slot = lax.rem(i, slots)

            @pl.when(i + 1 < count)
            def _():
                for copy in loads(i + 1, 1 - slot):
                    copy.start()

            for copy in data_loads(i, data[0], data[1]):
                copy.wait()
            arrived = loads(i, slot)
            for k, (acc, buf) in enumerate(zip(accs, (gbuf, dbuf, ubuf))):
                arrived[k].wait()
                if k != 1:
                    acc[...] += dot(feats[i, rows - tok :, :], buf[slot])
                else:
                    acc[...] += nt_dot(feats[i, : rows - tok, :], buf[slot])

            return 0

        lax.fori_loop(0, count, step, 0)

    any_spec = pl.BlockSpec(memory_space=pl.ANY)
    vmem = pl.BlockSpec(memory_space=pltpu.VMEM)
    args = pieces + [gate_w, up_w, down_w] + carried
    return pl.pallas_call(
        kernel,
        in_specs=[any_spec] * (2 * count + 3) + [vmem] * len(carried),
        out_specs=[vmem] * 3,
        out_shape=[jax.ShapeDtypeStruct(s, F32) for s in sum_shapes],
        scratch_shapes=[
            pltpu.VMEM((count, rows, width), BF16),
            pltpu.VMEM((slots, width, hidden), BF16),
            pltpu.VMEM((slots, width, hidden), BF16),
            pltpu.VMEM((slots, hidden, width), BF16),
            pltpu.SemaphoreType.DMA((2, count)),
            pltpu.SemaphoreType.DMA((3, slots)),
        ],
        input_output_aliases={2 * count + 3 + k: k for k in range(3)} if carried else {},
        compiler_params=pltpu.CompilerParams(vmem_limit_bytes=36 << 20),
        cost_estimate=pl.CostEstimate(
            flops=count * 2 * width * hidden * (rows + tok),
            transcendentals=0,
            bytes_accessed=count * width * (6 * hidden + 2 * rows),
        ),
        name="forward",
    )(*args)


def half_sigmoid(x):
    return 0.5 * jnp.tanh(x) + 0.5


def neuron_tile(theta, share, g, u, feeds):
    sig = half_sigmoid(0.5 * g)
    gs = g * sig
    current = gs * u
    usl = u * (sig * (1.0 + g * (1.0 - sig)))
    membrane = theta * share
    spikes = []
    for _ in feeds:
        pre = membrane + current
        spike = half_sigmoid((0.5 * slope_gain) * (pre - theta))
        spikes.append(spike)
        membrane = pre - theta * spike
    later = None
    for feed, spike in zip(feeds[::-1], spikes[::-1]):
        diff = feed if later is None else feed - later
        both = theta * diff * (slope_gain * spike * (1.0 - spike))
        dpre = both if later is None else both + later
        term = diff * spike - both
        dg = (dpre * usl).astype(BF16).astype(F32)
        du = (dpre * gs).astype(BF16).astype(F32)
        if later is None:
            grad, dgate, dup = term, dg, du
        else:
            grad, dgate, dup = grad + term, dgate + dg, dup + du
        later = dpre
    return dgate, dup, grad + later * share


def neuron_rows(gate, up, feed, lev_ref, off_ref, dg_ref, du_ref, gt_ref):
    tok, part = gate.shape
    steps = feed.shape[0] // tok
    tile = 16
    theta = jnp.broadcast_to(lev_ref[...].astype(F32) / 8.0, (tile, part))
    acc = jnp.zeros((tile, part), F32)
    for r in range(0, tok, tile):
        at = slice(r, r + tile)
        feeds = [feed[t * tok + r : t * tok + r + tile, :] for t in range(steps)]
        share = off_ref[at, :].astype(F32) / 256.0
        dgate, dup, grad = neuron_tile(theta, share, gate[at, :], up[at, :], feeds)
        dg_ref[at, :] = dgate.astype(BF16)
        du_ref[at, :] = dup.astype(BF16)
        acc = acc + grad
    gt_ref[...] = jnp.sum(acc, axis=0, keepdims=True)


def hidden_part(hidden):
    return 256 if hidden % 256 == 0 else hidden


def neuron_outs(tok, hidden):
    return [
        jax.ShapeDtypeStruct((tok, hidden), BF16),
        jax.ShapeDtypeStruct((tok, hidden), BF16),
        jax.ShapeDtypeStruct((1, hidden), F32),
    ]


def neuron_call(gate, up, feed, levels, offsets):
    tok, hidden = gate.shape
    part = hidden_part(hidden)
    col = lambda rows: pl.BlockSpec((rows, part), lambda s: (0, s))
    return pl.pallas_call(
        neuron_rows,
        grid=(hidden // part,),
        in_specs=[col(tok), col(tok), col(feed.shape[0]), col(1), col(tok)],
        out_specs=[col(tok), col(tok), col(1)],
        out_shape=neuron_outs(tok, hidden),
        name="neuron",
    )(gate, up, feed, levels.reshape(1, hidden), offsets)


def last_call(pair, blocks, gate_w, up_w, down_w, sums, levels, offsets):
    rows, width = pair[0].shape
    tok, hidden = sums[0].shape
    part = hidden_part(hidden)
    count = hidden // part

    def kernel(blk, own, other, ga, gb, ua, ub, da, db, gi, ui, fi, lev, off, dg, du, gt, gate, up, feed):
        now = lax.rem(pl.program_id(0), 2)
        neuron_rows(gate.at[1 - now], up.at[1 - now], feed.at[1 - now], lev, off, dg, du, gt)
        xo = own[rows - tok :, :]
        xp = other[rows - tok :, :]
        at = pl.ds(pl.multiple_of(jnp.minimum(pl.program_id(0), count - 1) * part, part), part)
        gate[now] = gi[:, at] + dot(xo, ga[...]) + dot(xp, gb[...])
        up[now] = ui[:, at] + dot(xo, ua[...]) + dot(xp, ub[...])
        feed[now] = fi[:, at] + nt_dot(own[: rows - tok, :], da[...]) + nt_dot(other[: rows - tok, :], db[...])

    ahead = lambda s: jnp.minimum(s, count - 1)
    behind = lambda s: jnp.maximum(s - 1, 0)
    whole = pl.BlockSpec((rows, width), lambda s, b: (0, 0))
    spec = lambda k: pl.BlockSpec((width, part), lambda s, b: (b[k, 0], ahead(s)))
    dspec = lambda k: pl.BlockSpec((part, width), lambda s, b: (ahead(s), b[k, 0]))
    late = lambda n: pl.BlockSpec((n, part), lambda s, b: (0, behind(s)))
    return pl.pallas_call(
        kernel,
        grid_spec=pltpu.PrefetchScalarGridSpec(
            num_scalar_prefetch=1,
            grid=(count + 1,),
            in_specs=[whole, whole, spec(0), spec(1), spec(0), spec(1), dspec(0), dspec(1)]
            + [pl.BlockSpec(memory_space=pltpu.VMEM)] * 3
            + [late(1), late(tok)],
            out_specs=[late(tok), late(tok), late(1)],
            scratch_shapes=[
                pltpu.VMEM((2, tok, part), F32),
                pltpu.VMEM((2, tok, part), F32),
                pltpu.VMEM((2, rows - tok, part), F32),
            ],
        ),
        out_shape=neuron_outs(tok, hidden),
        compiler_params=pltpu.CompilerParams(vmem_limit_bytes=28 << 20),
        name="last",
    )(blocks, *pair, gate_w, gate_w, up_w, up_w, down_w, down_w, *sums, levels.reshape(1, hidden), offsets)


def backward_call(dgate, dup, count, place, gate_w, up_w, width):
    tok, hidden = dgate.shape
    slots = 3

    def kernel(dg, du, gw, uw, out, gbuf, ubuf, sem):
        me = lax.axis_index(AXIS)

        def loads(i, slot):
            at = pl.multiple_of(place(me, i) * width, width)
            return (
                pltpu.make_async_copy(gw.at[pl.ds(at, width), :], gbuf.at[slot], sem.at[0, slot]),
                pltpu.make_async_copy(uw.at[pl.ds(at, width), :], ubuf.at[slot], sem.at[1, slot]),
            )

        for i in range(min(slots - 1, count)):
            for copy in loads(i, i):
                copy.start()

        def step(i, _):
            slot = lax.rem(i, slots)

            @pl.when(i + slots - 1 < count)
            def _():
                for copy in loads(i + slots - 1, lax.rem(i + slots - 1, slots)):
                    copy.start()

            for copy in loads(i, slot):
                copy.wait()
            out[i] = nt_dot(dg[...], gbuf[slot]) + nt_dot(du[...], ubuf[slot])
            return 0

        lax.fori_loop(0, count, step, 0)

    vmem = pl.BlockSpec(memory_space=pltpu.VMEM)
    any_spec = pl.BlockSpec(memory_space=pl.ANY)
    return pl.pallas_call(
        kernel,
        in_specs=[vmem, vmem, any_spec, any_spec],
        out_specs=vmem,
        out_shape=jax.ShapeDtypeStruct((count, tok, width), F32),
        scratch_shapes=[
            pltpu.VMEM((slots, width, hidden), BF16),
            pltpu.VMEM((slots, width, hidden), BF16),
            pltpu.SemaphoreType.DMA((2, slots)),
        ],
        compiler_params=pltpu.CompilerParams(vmem_limit_bytes=28 << 20),
        cost_estimate=pl.CostEstimate(
            flops=count * 4 * width * hidden * tok,
            transcendentals=0,
            bytes_accessed=count * width * (4 * hidden + 4 * tok),
        ),
        name="backward",
    )(dgate, dup, gate_w, up_w)


def z_map(moves):
    return [(i, moves[i // 4] * 4 + i % 4) for i in range(16) if i // 4 in moves]


CORE = [(i, i ^ 1) for i in range(16)]
PAIR = z_map({0: 1, 1: 0, 2: 3, 3: 2})
MID = z_map({1: 2, 2: 1})
OUT = z_map({1: 0, 2: 3})
CROSS = [(i, i ^ 2) for i in range(16)]


def around(turn, flip):
    return [(i, ((i // 4 + turn) % 4 * 4 + i % 4) ^ (2 * flip)) for i in range(16)]


def send(piece, moves):
    return lax.ppermute(piece, AXIS, moves)


fence = lax.optimization_barrier


def body_line(inputs, gate_w, up_w, down_w, cotangent, levels, offsets):
    steps, tok, width = cotangent.shape
    me = lax.axis_index(AXIS)
    core = me % 2
    chip = me // 2
    z = me // 4
    middle = (z == 1) | (z == 2)

    def blocks_of(chips):
        chips = jnp.stack(chips).astype(jnp.int32)
        return jnp.stack([2 * chips + core, 2 * chips + 1 - core]).astype(jnp.int32)

    own = jnp.concatenate([cotangent.reshape(steps * tok, width), inputs], axis=0)
    def far(me):
        inner = lax.rem(me // 4 + 1, 4) >= 2
        return jnp.where(inner, 6, 4), jnp.where(inner, 4, 6)

    def more(pairs, place, sums):
        return forward_call(tok, pairs, place, gate_w, up_w, down_w, sums)

    p1 = send(own, PAIR)
    p2a = send(own, MID)
    x0 = send(own, CROSS)
    own_c = send(own, CORE)
    sums = more([(own, own_c)], lambda me: [me // 2], None)
    p1, p2a, sums = fence((p1, p2a, sums))
    p2b = send(p1, MID)
    p3a = send(p2a, OUT)
    p1, x0 = fence((p1, x0))
    x1 = send(p1, CROSS)
    p1_c = send(p1, CORE)
    x0_c = send(x0, CORE)
    sums = more([(p1, p1_c), (x0, x0_c)], lambda me: [(me // 2) ^ 2, (me // 2) ^ 1], sums)
    p2b, p3a, p2a, sums = fence((p2b, p3a, p2a, sums))
    p3b = send(p2b, OUT)
    a = jnp.where(middle, p2a, p3a)
    a, x1 = fence((a, x1))
    x2 = send(a, CROSS)
    a_c = send(a, CORE)
    x1_c = send(x1, CORE)
    sums = more([(a, a_c), (x1, x1_c)], lambda me: [(me // 2) ^ far(me)[0], (me // 2) ^ 3], sums)
    p3b, p2b, sums = fence((p3b, p2b, sums))
    b = jnp.where(middle, p2b, p3b)
    b, x2 = fence((b, x2))
    x3 = send(b, CROSS)
    b_c = send(b, CORE)
    x2_c = send(x2, CORE)
    sums = more(
        [(b, b_c), (x2, x2_c)],
        lambda me: [(me // 2) ^ far(me)[1], (me // 2) ^ 1 ^ far(me)[0]],
        sums,
    )
    x3, sums = fence((x3, sums))
    x3_c = send(x3, CORE)
    dgate, dup, grad_threshold = last_call(
        (x3, x3_c), blocks_of([chip ^ 1 ^ far(me)[1]]), gate_w, up_w, down_w, sums, levels, offsets
    )

    turns = [2, 1, 3, 0]

    def partial(dgate, dup, flip):
        def place(me, i):
            k = lax.rem(i, 4)
            turn = jnp.where(k == 0, 2, jnp.where(k == 2, 3, jnp.where(k == 3, 0, 1)))
            to = (lax.rem(me // 4 + turn, 4) * 2 + lax.rem(me // 2, 2)) ^ flip
            return 2 * to + jnp.where(i < 4, 1 - lax.rem(me, 2), lax.rem(me, 2))

        out = backward_call(dgate, dup, 8, place, gate_w, up_w, width)
        return out[:4], out[4:]

    theirs, mine = partial(dgate, dup, 1)
    across = (mine + send(theirs, CORE)).astype(BF16)
    dgate, dup, across = fence((dgate, dup, across))
    across = send(across, CROSS)
    theirs, mine = partial(dgate, dup, 0)
    theirs, mine, across = fence((theirs, mine, across))
    column = mine + send(theirs, CORE) + across.astype(F32)
    grad_input = column[3]
    column = column.astype(BF16)
    for k in range(3):
        grad_input = grad_input + send(column[k], around(turns[k], 0)).astype(F32)
    return grad_input, grad_threshold.reshape(-1)


def body_plain(inputs, gate_w, up_w, down_w, cotangent, levels, offsets):
    steps, tok, width = cotangent.shape
    piece = lax.all_gather(inputs, AXIS, axis=1, tiled=True)
    gate = dot(piece, gate_w)
    up = dot(piece, up_w)
    cot = lax.all_gather(cotangent, AXIS, axis=2, tiled=True)
    feed = nt_dot(cot.reshape(steps * tok, -1), down_w)
    dgate, dup, grad_threshold = neuron_call(gate, up, feed, levels, offsets)
    term = nt_dot(dgate, gate_w) + nt_dot(dup, up_w)
    grad_input = lax.psum_scatter(term, AXIS, scatter_dimension=1, tiled=True)
    return grad_input, grad_threshold.reshape(-1)


def solution(mesh):
    placed = (
        P("groups", "tensor"),
        P(None, "tensor"),
        P(None, "tensor"),
        P("tensor", None),
        P(None, "groups", "tensor"),
        P("tensor"),
        P("groups", "tensor"),
    )
    body = body_line if mesh.shape[AXIS] == 16 else body_plain
    return jax.shard_map(
        body,
        mesh=mesh,
        in_specs=placed,
        out_specs=(P("groups", "tensor"), P(("groups", "tensor"))),
        check_vma=False,
    )
```

```python
import jax
import jax.numpy as jnp
from jax import lax
from jax.experimental import pallas as pl
from jax.experimental.pallas import tpu as pltpu
from jax.sharding import PartitionSpec as P

slope_gain = 4.0
AXIS = "tensor"
NT = (((1,), (1,)), ((), ()))
F32 = jnp.float32
BF16 = jnp.bfloat16


def nt_dot(left, weight):
    return lax.dot_general(left, weight, NT, preferred_element_type=F32)


def dot(left, right):
    return jnp.dot(left, right, preferred_element_type=F32)


def forward_call(tok, pairs, place, gate_w, up_w, down_w, sums):
    count = len(pairs)
    rows, half = pairs[0][0].shape
    width = 2 * half
    hidden = gate_w.shape[1]
    slots = 2
    pieces = [piece for pair in pairs for piece in pair]
    sum_shapes = [(tok, hidden), (tok, hidden), (rows - tok, hidden)]
    carried = [] if sums is None else list(sums)

    def kernel(*refs):
        me = lax.axis_index(AXIS)
        core = lax.rem(me, 2)
        chips = place(me)
        data = refs[: 2 * count]
        weights = refs[2 * count : 2 * count + 3]
        old = refs[2 * count + 3 : 2 * count + 3 + len(carried)]
        new = refs[2 * count + 3 + len(carried) : 2 * count + 6 + len(carried)]
        feats, gbuf, ubuf, dbuf, dsem, wsem = refs[2 * count + 6 + len(carried) :]
        gate, up, feed = new
        accs = (gate, feed, up)
        mine = pl.multiple_of(core * half, half)
        theirs = pl.multiple_of(half - core * half, half)

        def loads(i, slot):
            chip = chips[0]
            for j in range(1, count):
                chip = jnp.where(i == j, chips[j], chip)
            at = pl.multiple_of(chip * width, width)
            return (
                pltpu.make_async_copy(weights[0].at[pl.ds(at, width), :], gbuf.at[slot], wsem.at[0, slot]),
                pltpu.make_async_copy(weights[2].at[:, pl.ds(at, width)], dbuf.at[slot], wsem.at[2, slot]),
                pltpu.make_async_copy(weights[1].at[pl.ds(at, width), :], ubuf.at[slot], wsem.at[1, slot]),
            )

        def data_loads(j, own, other):
            return (
                pltpu.make_async_copy(own, feats.at[j, :, pl.ds(mine, half)], dsem.at[0, j]),
                pltpu.make_async_copy(other, feats.at[j, :, pl.ds(theirs, half)], dsem.at[1, j]),
            )

        for copy in data_loads(0, data[0], data[1]):
            copy.start()
        for copy in loads(0, 0):
            copy.start()
        for j in range(1, count):
            for copy in data_loads(j, data[2 * j], data[2 * j + 1]):
                copy.start()
        for k, acc in enumerate(new):
            acc[...] = old[k][...] if carried else jnp.zeros_like(acc)

        def step(i, _):
            slot = lax.rem(i, slots)

            @pl.when(i + 1 < count)
            def _():
                for copy in loads(i + 1, 1 - slot):
                    copy.start()

            for copy in data_loads(i, data[0], data[1]):
                copy.wait()
            arrived = loads(i, slot)
            for k, (acc, buf) in enumerate(zip(accs, (gbuf, dbuf, ubuf))):
                arrived[k].wait()
                if k != 1:
                    acc[...] += dot(feats[i, rows - tok :, :], buf[slot])
                else:
                    acc[...] += nt_dot(feats[i, : rows - tok, :], buf[slot])

            return 0

        lax.fori_loop(0, count, step, 0)

    any_spec = pl.BlockSpec(memory_space=pl.ANY)
    vmem = pl.BlockSpec(memory_space=pltpu.VMEM)
    args = pieces + [gate_w, up_w, down_w] + carried
    return pl.pallas_call(
        kernel,
        in_specs=[any_spec] * (2 * count + 3) + [vmem] * len(carried),
        out_specs=[vmem] * 3,
        out_shape=[jax.ShapeDtypeStruct(s, F32) for s in sum_shapes],
        scratch_shapes=[
            pltpu.VMEM((count, rows, width), BF16),
            pltpu.VMEM((slots, width, hidden), BF16),
            pltpu.VMEM((slots, width, hidden), BF16),
            pltpu.VMEM((slots, hidden, width), BF16),
            pltpu.SemaphoreType.DMA((2, count)),
            pltpu.SemaphoreType.DMA((3, slots)),
        ],
        input_output_aliases={2 * count + 3 + k: k for k in range(3)} if carried else {},
        compiler_params=pltpu.CompilerParams(vmem_limit_bytes=36 << 20),
        cost_estimate=pl.CostEstimate(
            flops=count * 2 * width * hidden * (rows + tok),
            transcendentals=0,
            bytes_accessed=count * width * (6 * hidden + 2 * rows),
        ),
        name="forward",
    )(*args)


def half_sigmoid(x):
    return 0.5 * jnp.tanh(x) + 0.5


def neuron_tile(theta, share, g, u, feeds):
    sig = half_sigmoid(0.5 * g)
    gs = g * sig
    current = gs * u
    usl = u * (sig * (1.0 + g * (1.0 - sig)))
    membrane = theta * share
    spikes = []
    for _ in feeds:
        pre = membrane + current
        spike = half_sigmoid((0.5 * slope_gain) * (pre - theta))
        spikes.append(spike)
        membrane = pre - theta * spike
    later = None
    for feed, spike in zip(feeds[::-1], spikes[::-1]):
        diff = feed if later is None else feed - later
        both = theta * diff * (slope_gain * spike * (1.0 - spike))
        dpre = both if later is None else both + later
        term = diff * spike - both
        dg = (dpre * usl).astype(BF16).astype(F32)
        du = (dpre * gs).astype(BF16).astype(F32)
        if later is None:
            grad, dgate, dup = term, dg, du
        else:
            grad, dgate, dup = grad + term, dgate + dg, dup + du
        later = dpre
    return dgate, dup, grad + later * share


def neuron_rows(gate, up, feed, lev_ref, off_ref, dg_ref, du_ref, gt_ref):
    tok, part = gate.shape
    steps = feed.shape[0] // tok
    tile = 16
    theta = jnp.broadcast_to(lev_ref[...].astype(F32) / 8.0, (tile, part))
    acc = jnp.zeros((tile, part), F32)
    for r in range(0, tok, tile):
        at = slice(r, r + tile)
        feeds = [feed[t * tok + r : t * tok + r + tile, :] for t in range(steps)]
        share = off_ref[at, :].astype(F32) / 256.0
        dgate, dup, grad = neuron_tile(theta, share, gate[at, :], up[at, :], feeds)
        dg_ref[at, :] = dgate.astype(BF16)
        du_ref[at, :] = dup.astype(BF16)
        acc = acc + grad
    gt_ref[...] = jnp.sum(acc, axis=0, keepdims=True)


def hidden_part(hidden):
    return 256 if hidden % 256 == 0 else hidden


def neuron_outs(tok, hidden):
    return [
        jax.ShapeDtypeStruct((tok, hidden), BF16),
        jax.ShapeDtypeStruct((tok, hidden), BF16),
        jax.ShapeDtypeStruct((1, hidden), F32),
    ]


def neuron_call(gate, up, feed, levels, offsets):
    tok, hidden = gate.shape
    part = hidden_part(hidden)
    col = lambda rows: pl.BlockSpec((rows, part), lambda s: (0, s))
    return pl.pallas_call(
        neuron_rows,
        grid=(hidden // part,),
        in_specs=[col(tok), col(tok), col(feed.shape[0]), col(1), col(tok)],
        out_specs=[col(tok), col(tok), col(1)],
        out_shape=neuron_outs(tok, hidden),
        name="neuron",
    )(gate, up, feed, levels.reshape(1, hidden), offsets)


def last_call(pair, place, gate_w, up_w, down_w, sums, levels, offsets):
    rows, half = pair[0].shape
    width = 2 * half
    tok, hidden = sums[0].shape
    part = hidden_part(hidden)
    count = hidden // part
    ahead = 2

    def kernel(
        own, other, gw, uw, dw, gi, ui, fi, lev, off, dg, du, gt,
        feats, gbuf, ubuf, dbuf, gate, up, feed, dsem, wsem,
    ):
        me = lax.axis_index(AXIS)
        core = lax.rem(me, 2)
        at = pl.multiple_of(place(me) * width, width)
        mine = pl.multiple_of(core * half, half)
        theirs = pl.multiple_of(half - core * half, half)
        data = (
            pltpu.make_async_copy(own, feats.at[:, pl.ds(mine, half)], dsem.at[0]),
            pltpu.make_async_copy(other, feats.at[:, pl.ds(theirs, half)], dsem.at[1]),
        )

        def loads(s):
            cols = pl.ds(pl.multiple_of(s * part, part), part)
            return (
                pltpu.make_async_copy(gw.at[pl.ds(at, width), cols], gbuf.at[s], wsem.at[0, s]),
                pltpu.make_async_copy(uw.at[pl.ds(at, width), cols], ubuf.at[s], wsem.at[1, s]),
                pltpu.make_async_copy(dw.at[cols, pl.ds(at, width)], dbuf.at[s], wsem.at[2, s]),
            )

        for copy in data:
            copy.start()
        for s in range(min(ahead, count)):
            for copy in loads(s):
                copy.start()
        for copy in data:
            copy.wait()

        def step(s, _):
            @pl.when(s + ahead < count)
            def _():
                for copy in loads(s + ahead):
                    copy.start()

            cols = pl.ds(pl.multiple_of(s * part, part), part)
            for copy in loads(s):
                copy.wait()
            gate[...] = gi[:, cols] + dot(feats[rows - tok :, :], gbuf[s])
            up[...] = ui[:, cols] + dot(feats[rows - tok :, :], ubuf[s])
            feed[...] = fi[:, cols] + nt_dot(feats[: rows - tok, :], dbuf[s])
            neuron_rows(
                gate, up, feed, lev.at[:, cols], off.at[:, cols], dg.at[:, cols], du.at[:, cols], gt.at[:, cols]
            )
            return 0

        lax.fori_loop(0, count, step, 0)

    any_spec = pl.BlockSpec(memory_space=pl.ANY)
    vmem = pl.BlockSpec(memory_space=pltpu.VMEM)
    return pl.pallas_call(
        kernel,
        in_specs=[any_spec] * 5 + [vmem] * 5,
        out_specs=[vmem] * 3,
        out_shape=neuron_outs(tok, hidden),
        scratch_shapes=[
            pltpu.VMEM((rows, width), BF16),
            pltpu.VMEM((count, width, part), BF16),
            pltpu.VMEM((count, width, part), BF16),
            pltpu.VMEM((count, part, width), BF16),
            pltpu.VMEM((tok, part), F32),
            pltpu.VMEM((tok, part), F32),
            pltpu.VMEM((rows - tok, part), F32),
            pltpu.SemaphoreType.DMA((2,)),
            pltpu.SemaphoreType.DMA((3, count)),
        ],
        compiler_params=pltpu.CompilerParams(vmem_limit_bytes=28 << 20),
        name="last",
    )(*pair, gate_w, up_w, down_w, *sums, levels.reshape(1, hidden), offsets)


def backward_call(dgate, dup, count, place, gate_w, up_w, width):
    tok, hidden = dgate.shape
    slots = 3

    def kernel(dg, du, gw, uw, out, gbuf, ubuf, sem):
        me = lax.axis_index(AXIS)

        def loads(i, slot):
            at = pl.multiple_of(place(me, i) * width, width)
            return (
                pltpu.make_async_copy(gw.at[pl.ds(at, width), :], gbuf.at[slot], sem.at[0, slot]),
                pltpu.make_async_copy(uw.at[pl.ds(at, width), :], ubuf.at[slot], sem.at[1, slot]),
            )

        for i in range(min(slots - 1, count)):
            for copy in loads(i, i):
                copy.start()

        def step(i, _):
            slot = lax.rem(i, slots)

            @pl.when(i + slots - 1 < count)
            def _():
                for copy in loads(i + slots - 1, lax.rem(i + slots - 1, slots)):
                    copy.start()

            for copy in loads(i, slot):
                copy.wait()
            out[i] = nt_dot(dg[...], gbuf[slot]) + nt_dot(du[...], ubuf[slot])
            return 0

        lax.fori_loop(0, count, step, 0)

    vmem = pl.BlockSpec(memory_space=pltpu.VMEM)
    any_spec = pl.BlockSpec(memory_space=pl.ANY)
    return pl.pallas_call(
        kernel,
        in_specs=[vmem, vmem, any_spec, any_spec],
        out_specs=vmem,
        out_shape=jax.ShapeDtypeStruct((count, tok, width), F32),
        scratch_shapes=[
            pltpu.VMEM((slots, width, hidden), BF16),
            pltpu.VMEM((slots, width, hidden), BF16),
            pltpu.SemaphoreType.DMA((2, slots)),
        ],
        compiler_params=pltpu.CompilerParams(vmem_limit_bytes=28 << 20),
        cost_estimate=pl.CostEstimate(
            flops=count * 4 * width * hidden * tok,
            transcendentals=0,
            bytes_accessed=count * width * (4 * hidden + 4 * tok),
        ),
        name="backward",
    )(dgate, dup, gate_w, up_w)


def z_map(moves):
    return [(i, moves[i // 4] * 4 + i % 4) for i in range(16) if i // 4 in moves]


CORE = [(i, i ^ 1) for i in range(16)]
PAIR = z_map({0: 1, 1: 0, 2: 3, 3: 2})
MID = z_map({1: 2, 2: 1})
OUT = z_map({1: 0, 2: 3})
CROSS = [(i, i ^ 2) for i in range(16)]


def around(turn, flip):
    return [(i, ((i // 4 + turn) % 4 * 4 + i % 4) ^ (2 * flip)) for i in range(16)]


def send(piece, moves):
    return lax.ppermute(piece, AXIS, moves)


fence = lax.optimization_barrier


def body_line(inputs, gate_w, up_w, down_w, cotangent, levels, offsets):
    steps, tok, width = cotangent.shape
    me = lax.axis_index(AXIS)
    z = me // 4
    middle = (z == 1) | (z == 2)

    own = jnp.concatenate([cotangent.reshape(steps * tok, width), inputs], axis=0)
    def far(me):
        inner = lax.rem(me // 4 + 1, 4) >= 2
        return jnp.where(inner, 6, 4), jnp.where(inner, 4, 6)

    def more(pairs, place, sums):
        return forward_call(tok, pairs, place, gate_w, up_w, down_w, sums)

    p1 = send(own, PAIR)
    p2a = send(own, MID)
    x0 = send(own, CROSS)
    own_c = send(own, CORE)
    sums = more([(own, own_c)], lambda me: [me // 2], None)
    p1, p2a, sums = fence((p1, p2a, sums))
    p2b = send(p1, MID)
    p3a = send(p2a, OUT)
    p1, x0 = fence((p1, x0))
    x1 = send(p1, CROSS)
    p1_c = send(p1, CORE)
    x0_c = send(x0, CORE)
    sums = more([(p1, p1_c), (x0, x0_c)], lambda me: [(me // 2) ^ 2, (me // 2) ^ 1], sums)
    p2b, p3a, p2a, sums = fence((p2b, p3a, p2a, sums))
    p3b = send(p2b, OUT)
    a = jnp.where(middle, p2a, p3a)
    a, x1 = fence((a, x1))
    x2 = send(a, CROSS)
    a_c = send(a, CORE)
    x1_c = send(x1, CORE)
    sums = more([(a, a_c), (x1, x1_c)], lambda me: [(me // 2) ^ far(me)[0], (me // 2) ^ 3], sums)
    p3b, p2b, sums = fence((p3b, p2b, sums))
    b = jnp.where(middle, p2b, p3b)
    b, x2 = fence((b, x2))
    x3 = send(b, CROSS)
    b_c = send(b, CORE)
    x2_c = send(x2, CORE)
    sums = more(
        [(b, b_c), (x2, x2_c)],
        lambda me: [(me // 2) ^ far(me)[1], (me // 2) ^ 1 ^ far(me)[0]],
        sums,
    )
    x3, sums = fence((x3, sums))
    x3_c = send(x3, CORE)
    dgate, dup, grad_threshold = last_call(
        (x3, x3_c), lambda me: (me // 2) ^ 1 ^ far(me)[1], gate_w, up_w, down_w, sums, levels, offsets
    )

    turns = [2, 1, 3, 0]

    def partial(dgate, dup, flip):
        def place(me, i):
            k = lax.rem(i, 4)
            turn = jnp.where(k == 0, 2, jnp.where(k == 2, 3, jnp.where(k == 3, 0, 1)))
            to = (lax.rem(me // 4 + turn, 4) * 2 + lax.rem(me // 2, 2)) ^ flip
            return 2 * to + jnp.where(i < 4, 1 - lax.rem(me, 2), lax.rem(me, 2))

        out = backward_call(dgate, dup, 8, place, gate_w, up_w, width)
        return out[:4], out[4:]

    theirs, mine = partial(dgate, dup, 1)
    across = (mine + send(theirs, CORE)).astype(BF16)
    dgate, dup, across = fence((dgate, dup, across))
    across = send(across, CROSS)
    theirs, mine = partial(dgate, dup, 0)
    theirs, mine, across = fence((theirs, mine, across))
    column = mine + send(theirs, CORE) + across.astype(F32)
    grad_input = column[3]
    column = column.astype(BF16)
    for k in range(3):
        grad_input = grad_input + send(column[k], around(turns[k], 0)).astype(F32)
    return grad_input, grad_threshold.reshape(-1)


def body_plain(inputs, gate_w, up_w, down_w, cotangent, levels, offsets):
    steps, tok, width = cotangent.shape
    piece = lax.all_gather(inputs, AXIS, axis=1, tiled=True)
    gate = dot(piece, gate_w)
    up = dot(piece, up_w)
    cot = lax.all_gather(cotangent, AXIS, axis=2, tiled=True)
    feed = nt_dot(cot.reshape(steps * tok, -1), down_w)
    dgate, dup, grad_threshold = neuron_call(gate, up, feed, levels, offsets)
    term = nt_dot(dgate, gate_w) + nt_dot(dup, up_w)
    grad_input = lax.psum_scatter(term, AXIS, scatter_dimension=1, tiled=True)
    return grad_input, grad_threshold.reshape(-1)


def solution(mesh):
    placed = (
        P("groups", "tensor"),
        P(None, "tensor"),
        P(None, "tensor"),
        P("tensor", None),
        P(None, "groups", "tensor"),
        P("tensor"),
        P("groups", "tensor"),
    )
    body = body_line if mesh.shape[AXIS] == 16 else body_plain
    return jax.shard_map(
        body,
        mesh=mesh,
        in_specs=placed,
        out_specs=(P("groups", "tensor"), P(("groups", "tensor"))),
        check_vma=False,
    )
```

```python
import jax
import jax.numpy as jnp
from jax import lax
from jax.experimental import pallas as pl
from jax.experimental.pallas import tpu as pltpu
from jax.sharding import PartitionSpec as P

slope_gain = 4.0
AXIS = "tensor"
NT = (((1,), (1,)), ((), ()))
F32 = jnp.float32
BF16 = jnp.bfloat16


def nt_dot(left, weight):
    return lax.dot_general(left, weight, NT, preferred_element_type=F32)


def dot(left, right):
    return jnp.dot(left, right, preferred_element_type=F32)


def forward_call(tok, pairs, place, gate_w, up_w, down_w, sums):
    count = len(pairs)
    rows, half = pairs[0][0].shape
    width = 2 * half
    hidden = gate_w.shape[1]
    slots = 2
    pieces = [piece for pair in pairs for piece in pair]
    sum_shapes = [(tok, hidden), (tok, hidden), (rows - tok, hidden)]
    carried = [] if sums is None else list(sums)

    def kernel(*refs):
        me = lax.axis_index(AXIS)
        core = lax.rem(me, 2)
        chips = place(me)
        data = refs[: 2 * count]
        weights = refs[2 * count : 2 * count + 3]
        old = refs[2 * count + 3 : 2 * count + 3 + len(carried)]
        new = refs[2 * count + 3 + len(carried) : 2 * count + 6 + len(carried)]
        feats, gbuf, ubuf, dbuf, dsem, wsem = refs[2 * count + 6 + len(carried) :]
        gate, up, feed = new
        accs = (gate, feed, up)
        mine = pl.multiple_of(core * half, half)
        theirs = pl.multiple_of(half - core * half, half)

        def loads(i, slot):
            chip = chips[0]
            for j in range(1, count):
                chip = jnp.where(i == j, chips[j], chip)
            at = pl.multiple_of(chip * width, width)
            return (
                pltpu.make_async_copy(weights[0].at[pl.ds(at, width), :], gbuf.at[slot], wsem.at[0, slot]),
                pltpu.make_async_copy(weights[2].at[:, pl.ds(at, width)], dbuf.at[slot], wsem.at[2, slot]),
                pltpu.make_async_copy(weights[1].at[pl.ds(at, width), :], ubuf.at[slot], wsem.at[1, slot]),
            )

        def data_loads(j, own, other):
            return (
                pltpu.make_async_copy(own, feats.at[j, :, pl.ds(mine, half)], dsem.at[0, j]),
                pltpu.make_async_copy(other, feats.at[j, :, pl.ds(theirs, half)], dsem.at[1, j]),
            )

        for copy in data_loads(0, data[0], data[1]):
            copy.start()
        for copy in loads(0, 0):
            copy.start()
        for j in range(1, count):
            for copy in data_loads(j, data[2 * j], data[2 * j + 1]):
                copy.start()
        for k, acc in enumerate(new):
            acc[...] = old[k][...] if carried else jnp.zeros_like(acc)

        def step(i, _):
            slot = lax.rem(i, slots)

            @pl.when(i + 1 < count)
            def _():
                for copy in loads(i + 1, 1 - slot):
                    copy.start()

            for copy in data_loads(i, data[0], data[1]):
                copy.wait()
            arrived = loads(i, slot)
            for k, (acc, buf) in enumerate(zip(accs, (gbuf, dbuf, ubuf))):
                arrived[k].wait()
                if k != 1:
                    acc[...] += dot(feats[i, rows - tok :, :], buf[slot])
                else:
                    acc[...] += nt_dot(feats[i, : rows - tok, :], buf[slot])

            return 0

        lax.fori_loop(0, count, step, 0)

    any_spec = pl.BlockSpec(memory_space=pl.ANY)
    vmem = pl.BlockSpec(memory_space=pltpu.VMEM)
    args = pieces + [gate_w, up_w, down_w] + carried
    return pl.pallas_call(
        kernel,
        in_specs=[any_spec] * (2 * count + 3) + [vmem] * len(carried),
        out_specs=[vmem] * 3,
        out_shape=[jax.ShapeDtypeStruct(s, F32) for s in sum_shapes],
        scratch_shapes=[
            pltpu.VMEM((count, rows, width), BF16),
            pltpu.VMEM((slots, width, hidden), BF16),
            pltpu.VMEM((slots, width, hidden), BF16),
            pltpu.VMEM((slots, hidden, width), BF16),
            pltpu.SemaphoreType.DMA((2, count)),
            pltpu.SemaphoreType.DMA((3, slots)),
        ],
        input_output_aliases={2 * count + 3 + k: k for k in range(3)} if carried else {},
        compiler_params=pltpu.CompilerParams(vmem_limit_bytes=36 << 20),
        cost_estimate=pl.CostEstimate(
            flops=count * 2 * width * hidden * (rows + tok),
            transcendentals=0,
            bytes_accessed=count * width * (6 * hidden + 2 * rows),
        ),
        name="forward",
    )(*args)


def half_sigmoid(x):
    return 0.5 * jnp.tanh(x) + 0.5


def neuron_tile(theta, share, g, u, feeds):
    sig = half_sigmoid(0.5 * g)
    gs = g * sig
    current = gs * u
    usl = u * (sig * (1.0 + g * (1.0 - sig)))
    membrane = theta * share
    spikes = []
    for _ in feeds:
        pre = membrane + current
        spike = half_sigmoid((0.5 * slope_gain) * (pre - theta))
        spikes.append(spike)
        membrane = pre - theta * spike
    later = None
    for feed, spike in zip(feeds[::-1], spikes[::-1]):
        diff = feed if later is None else feed - later
        both = theta * diff * (slope_gain * spike * (1.0 - spike))
        dpre = both if later is None else both + later
        term = diff * spike - both
        dg = (dpre * usl).astype(BF16).astype(F32)
        du = (dpre * gs).astype(BF16).astype(F32)
        if later is None:
            grad, dgate, dup = term, dg, du
        else:
            grad, dgate, dup = grad + term, dgate + dg, dup + du
        later = dpre
    return dgate, dup, grad + later * share


def neuron_rows(gate, up, feed, lev_ref, off_ref, dg_ref, du_ref, gt_ref):
    tok, part = gate.shape
    steps = feed.shape[0] // tok
    tile = 16
    theta = jnp.broadcast_to(lev_ref[...].astype(F32) / 8.0, (tile, part))
    acc = jnp.zeros((tile, part), F32)
    for r in range(0, tok, tile):
        at = slice(r, r + tile)
        feeds = [feed[t * tok + r : t * tok + r + tile, :] for t in range(steps)]
        share = off_ref[at, :].astype(F32) / 256.0
        dgate, dup, grad = neuron_tile(theta, share, gate[at, :], up[at, :], feeds)
        dg_ref[at, :] = dgate.astype(BF16)
        du_ref[at, :] = dup.astype(BF16)
        acc = acc + grad
    gt_ref[...] = jnp.sum(acc, axis=0, keepdims=True)


def hidden_part(hidden):
    return 256 if hidden % 256 == 0 else hidden


def neuron_outs(tok, hidden):
    return [
        jax.ShapeDtypeStruct((tok, hidden), BF16),
        jax.ShapeDtypeStruct((tok, hidden), BF16),
        jax.ShapeDtypeStruct((1, hidden), F32),
    ]


def neuron_call(gate, up, feed, levels, offsets):
    tok, hidden = gate.shape
    part = hidden_part(hidden)
    col = lambda rows: pl.BlockSpec((rows, part), lambda s: (0, s))
    return pl.pallas_call(
        neuron_rows,
        grid=(hidden // part,),
        in_specs=[col(tok), col(tok), col(feed.shape[0]), col(1), col(tok)],
        out_specs=[col(tok), col(tok), col(1)],
        out_shape=neuron_outs(tok, hidden),
        name="neuron",
    )(gate, up, feed, levels.reshape(1, hidden), offsets)


def last_call(pair, place, gate_w, up_w, down_w, sums, levels, offsets):
    rows, half = pair[0].shape
    width = 2 * half
    tok, hidden = sums[0].shape
    part = hidden_part(hidden)
    count = hidden // part
    ahead = 2

    def kernel(
        own, other, gw, uw, dw, gi, ui, fi, lev, off, dg, du, gt,
        feats, gbuf, ubuf, dbuf, gate, up, feed, dsem, wsem,
    ):
        me = lax.axis_index(AXIS)
        core = lax.rem(me, 2)
        at = pl.multiple_of(place(me) * width, width)
        mine = pl.multiple_of(core * half, half)
        theirs = pl.multiple_of(half - core * half, half)
        data = (
            pltpu.make_async_copy(own, feats.at[:, pl.ds(mine, half)], dsem.at[0]),
            pltpu.make_async_copy(other, feats.at[:, pl.ds(theirs, half)], dsem.at[1]),
        )

        def loads(s):
            cols = pl.ds(pl.multiple_of(s * part, part), part)
            return (
                pltpu.make_async_copy(gw.at[pl.ds(at, width), cols], gbuf.at[s], wsem.at[0, s]),
                pltpu.make_async_copy(uw.at[pl.ds(at, width), cols], ubuf.at[s], wsem.at[1, s]),
                pltpu.make_async_copy(dw.at[cols, pl.ds(at, width)], dbuf.at[s], wsem.at[2, s]),
            )

        for copy in data:
            copy.start()
        for s in range(min(ahead, count)):
            for copy in loads(s):
                copy.start()
        for copy in data:
            copy.wait()

        def step(s, _):
            @pl.when(s + ahead < count)
            def _():
                for copy in loads(s + ahead):
                    copy.start()

            cols = pl.ds(pl.multiple_of(s * part, part), part)
            for copy in loads(s):
                copy.wait()
            gate[...] = gi[:, cols] + dot(feats[rows - tok :, :], gbuf[s])
            up[...] = ui[:, cols] + dot(feats[rows - tok :, :], ubuf[s])
            feed[...] = fi[:, cols] + nt_dot(feats[: rows - tok, :], dbuf[s])
            neuron_rows(
                gate, up, feed, lev.at[:, cols], off.at[:, cols], dg.at[:, cols], du.at[:, cols], gt.at[:, cols]
            )
            return 0

        lax.fori_loop(0, count, step, 0)

    any_spec = pl.BlockSpec(memory_space=pl.ANY)
    vmem = pl.BlockSpec(memory_space=pltpu.VMEM)
    return pl.pallas_call(
        kernel,
        in_specs=[any_spec] * 5 + [vmem] * 5,
        out_specs=[vmem] * 3,
        out_shape=neuron_outs(tok, hidden),
        scratch_shapes=[
            pltpu.VMEM((rows, width), BF16),
            pltpu.VMEM((count, width, part), BF16),
            pltpu.VMEM((count, width, part), BF16),
            pltpu.VMEM((count, part, width), BF16),
            pltpu.VMEM((tok, part), F32),
            pltpu.VMEM((tok, part), F32),
            pltpu.VMEM((rows - tok, part), F32),
            pltpu.SemaphoreType.DMA((2,)),
            pltpu.SemaphoreType.DMA((3, count)),
        ],
        compiler_params=pltpu.CompilerParams(vmem_limit_bytes=28 << 20),
        name="last",
    )(*pair, gate_w, up_w, down_w, *sums, levels.reshape(1, hidden), offsets)


def backward_call(dgate, dup, count, place, gate_w, up_w, width):
    tok, hidden = dgate.shape
    slots = 3

    def kernel(dg, du, gw, uw, out, gbuf, ubuf, sem):
        me = lax.axis_index(AXIS)

        def loads(i, slot):
            at = pl.multiple_of(place(me, i) * width, width)
            return (
                pltpu.make_async_copy(gw.at[pl.ds(at, width), :], gbuf.at[slot], sem.at[0, slot]),
                pltpu.make_async_copy(uw.at[pl.ds(at, width), :], ubuf.at[slot], sem.at[1, slot]),
            )

        for i in range(min(slots - 1, count)):
            for copy in loads(i, i):
                copy.start()

        def step(i, _):
            slot = lax.rem(i, slots)

            @pl.when(i + slots - 1 < count)
            def _():
                for copy in loads(i + slots - 1, lax.rem(i + slots - 1, slots)):
                    copy.start()

            for copy in loads(i, slot):
                copy.wait()
            out[i] = nt_dot(dg[...], gbuf[slot]) + nt_dot(du[...], ubuf[slot])
            return 0

        lax.fori_loop(0, count, step, 0)

    vmem = pl.BlockSpec(memory_space=pltpu.VMEM)
    any_spec = pl.BlockSpec(memory_space=pl.ANY)
    return pl.pallas_call(
        kernel,
        in_specs=[vmem, vmem, any_spec, any_spec],
        out_specs=vmem,
        out_shape=jax.ShapeDtypeStruct((count, tok, width), F32),
        scratch_shapes=[
            pltpu.VMEM((slots, width, hidden), BF16),
            pltpu.VMEM((slots, width, hidden), BF16),
            pltpu.SemaphoreType.DMA((2, slots)),
        ],
        compiler_params=pltpu.CompilerParams(vmem_limit_bytes=28 << 20),
        cost_estimate=pl.CostEstimate(
            flops=count * 4 * width * hidden * tok,
            transcendentals=0,
            bytes_accessed=count * width * (4 * hidden + 4 * tok),
        ),
        name="backward",
    )(dgate, dup, gate_w, up_w)


def z_map(moves):
    return [(i, moves[i // 4] * 4 + i % 4) for i in range(16) if i // 4 in moves]


CORE = [(i, i ^ 1) for i in range(16)]
PAIR = z_map({0: 1, 1: 0, 2: 3, 3: 2})
MID = z_map({1: 2, 2: 1})
OUT = z_map({1: 0, 2: 3})
CROSS = [(i, i ^ 2) for i in range(16)]


def exchanged(turn):
    return [(i, i ^ (4 * turn)) for i in range(16)]


def send(piece, moves):
    return lax.ppermute(piece, AXIS, moves)


fence = lax.optimization_barrier


def body_line(inputs, gate_w, up_w, down_w, cotangent, levels, offsets):
    steps, tok, width = cotangent.shape
    me = lax.axis_index(AXIS)
    z = me // 4
    middle = (z == 1) | (z == 2)

    own = jnp.concatenate([cotangent.reshape(steps * tok, width), inputs], axis=0)
    def far(me):
        inner = lax.rem(me // 4 + 1, 4) >= 2
        return jnp.where(inner, 6, 4), jnp.where(inner, 4, 6)

    def more(pairs, place, sums):
        return forward_call(tok, pairs, place, gate_w, up_w, down_w, sums)

    p1 = send(own, PAIR)
    p2a = send(own, MID)
    x0 = send(own, CROSS)
    own_c = send(own, CORE)
    sums = more([(own, own_c)], lambda me: [me // 2], None)
    p1, p2a, sums = fence((p1, p2a, sums))
    p2b = send(p1, MID)
    p3a = send(p2a, OUT)
    p1, x0 = fence((p1, x0))
    x1 = send(p1, CROSS)
    p1_c = send(p1, CORE)
    x0_c = send(x0, CORE)
    sums = more([(p1, p1_c), (x0, x0_c)], lambda me: [(me // 2) ^ 2, (me // 2) ^ 1], sums)
    p2b, p3a, p2a, sums = fence((p2b, p3a, p2a, sums))
    p3b = send(p2b, OUT)
    a = jnp.where(middle, p2a, p3a)
    a, x1 = fence((a, x1))
    x2 = send(a, CROSS)
    a_c = send(a, CORE)
    x1_c = send(x1, CORE)
    sums = more([(a, a_c), (x1, x1_c)], lambda me: [(me // 2) ^ far(me)[0], (me // 2) ^ 3], sums)
    p3b, p2b, sums = fence((p3b, p2b, sums))
    b = jnp.where(middle, p2b, p3b)
    b, x2 = fence((b, x2))
    x3 = send(b, CROSS)
    b_c = send(b, CORE)
    x2_c = send(x2, CORE)
    sums = more(
        [(b, b_c), (x2, x2_c)],
        lambda me: [(me // 2) ^ far(me)[1], (me // 2) ^ 1 ^ far(me)[0]],
        sums,
    )
    x3, sums = fence((x3, sums))
    x3_c = send(x3, CORE)
    dgate, dup, grad_threshold = last_call(
        (x3, x3_c), lambda me: (me // 2) ^ 1 ^ far(me)[1], gate_w, up_w, down_w, sums, levels, offsets
    )

    turns = [3, 2, 1, 0]

    def partial(dgate, dup, flip):
        def place(me, i):
            k = lax.rem(i, 4)
            to = (((me // 4) ^ (3 - k)) * 2 + lax.rem(me // 2, 2)) ^ flip
            return 2 * to + jnp.where(i < 4, 1 - lax.rem(me, 2), lax.rem(me, 2))

        out = backward_call(dgate, dup, 8, place, gate_w, up_w, width)
        return out[:4], out[4:]

    theirs, mine = partial(dgate, dup, 1)
    across = (mine + send(theirs, CORE)).astype(BF16)
    dgate, dup, across = fence((dgate, dup, across))
    across = send(across, CROSS)
    theirs, mine = partial(dgate, dup, 0)
    theirs, mine, across = fence((theirs, mine, across))
    column = mine + send(theirs, CORE) + across.astype(F32)
    grad_input = column[3]
    column = column.astype(BF16)
    for k in range(3):
        grad_input = grad_input + send(column[k], exchanged(turns[k])).astype(F32)
    return grad_input, grad_threshold.reshape(-1)


def body_plain(inputs, gate_w, up_w, down_w, cotangent, levels, offsets):
    steps, tok, width = cotangent.shape
    piece = lax.all_gather(inputs, AXIS, axis=1, tiled=True)
    gate = dot(piece, gate_w)
    up = dot(piece, up_w)
    cot = lax.all_gather(cotangent, AXIS, axis=2, tiled=True)
    feed = nt_dot(cot.reshape(steps * tok, -1), down_w)
    dgate, dup, grad_threshold = neuron_call(gate, up, feed, levels, offsets)
    term = nt_dot(dgate, gate_w) + nt_dot(dup, up_w)
    grad_input = lax.psum_scatter(term, AXIS, scatter_dimension=1, tiled=True)
    return grad_input, grad_threshold.reshape(-1)


def solution(mesh):
    placed = (
        P("groups", "tensor"),
        P(None, "tensor"),
        P(None, "tensor"),
        P("tensor", None),
        P(None, "groups", "tensor"),
        P("tensor"),
        P("groups", "tensor"),
    )
    body = body_line if mesh.shape[AXIS] == 16 else body_plain
    return jax.shard_map(
        body,
        mesh=mesh,
        in_specs=placed,
        out_specs=(P("groups", "tensor"), P(("groups", "tensor"))),
        check_vma=False,
    )
```
